128 devices in a mesh: dp: 8 (over z, y_hi), tensor: 16 (over y_lo, x, core).
Axes of the slice: x: 4, y: 4 (y_hi: 2, y_lo: 2; y = y_hi * 2 + y_lo), z: 4, core: 2. Of those that a mesh axis runs over, the one named last changes fastest.
Arguments:
- inputs: bfloat16 [16384, 2048], P(('dp', 'tensor')), may hold values from -24 to 24
- grad_out: bfloat16 [16384, 2048], P(('dp', 'tensor')), may hold values from -24 to 24
- gate_pre: bfloat16 [16384, 6144], P('dp', 'tensor'), may hold values from -6 to 6
- up_pre: bfloat16 [16384, 6144], P('dp', 'tensor'), may hold values from -6 to 6
- w_gate: bfloat16 [2048, 6144], P(None, 'tensor'), may hold values from -0.125 to 0.125
- w_up: bfloat16 [2048, 6144], P(None, 'tensor'), may hold values from -0.125 to 0.125
- w_down: bfloat16 [6144, 2048], P('tensor'), may hold values from -0.078125 to 0.078125
Outputs:
- d_input: float32 [16384, 2048], P(('dp', 'tensor'))
- grad_gate: float32 [2048, 6144], P('dp', 'tensor')
- grad_up: float32 [2048, 6144], P('dp', 'tensor')
- grad_down: float32 [6144, 2048], P('tensor', 'dp')
The draws below stay inside these ranges and needn't reach their ends.
All inputs are finite; a program needn't handle non-finite values.
Results may differ from the reference program's by a relative error of at most 0.0029.
Values may be sent and summed in bfloat16 or wider, within the bound.
No kernel may reach another device: no remote copies, remote signals or barrier semaphores. Data moves between devices by JAX's collectives and lax.ppermute only.
A program may use at most 128 MiB of HBM per device.

```python
import jax
import jax.numpy as jnp

D = 2048
FF = 6144
TOKENS = 16384


def raised(result, key, source, target, parts, factor):
    def block_of(axis_at):
        return (jnp.arange(result.shape[axis_at]) // (result.shape[axis_at] // parts)).reshape((-1,) + (1,) * (result.ndim - 1 - axis_at))

    first = jax.random.permutation(key, parts)[block_of(target)]
    second = (block_of(target) + parts // 2) % parts
    return jnp.where((block_of(source) == first) | (block_of(source) == second), factor * result, result)


def shard_levels(stream_key, shape, split, smallest, high):
    level = 1.0
    for position, shards_of in split:
        steps = jax.random.uniform(jax.random.fold_in(jax.random.fold_in(stream_key, 6), position), (shards_of,), jnp.float32, smallest / len(split), high / len(split))
        level = level * jnp.repeat(jnp.exp(steps), shape[position] // shards_of).reshape((-1,) + (1,) * (len(shape) - 1 - position))
    return level


def centred(rng, dims, deviation, most, shards=(), kind=jnp.bfloat16):
    values = deviation * jax.random.normal(rng, dims, jnp.float32)
    if shards:
        values = values * shard_levels(rng, dims, shards, -0.22, 0.18)
    return jnp.clip(values, -most, most).astype(kind)


def heavy_noise(own_key, dims, width, reach, pieces, heavy, held_as=jnp.bfloat16):
    result = width * jax.random.normal(own_key, dims, jnp.float32)
    if pieces:
        result = result * shard_levels(own_key, dims, pieces, -0.22, 0.18)
    return jnp.clip(raised(result, jax.random.fold_in(own_key, 3), *heavy), -reach, reach).astype(held_as)


def setup_inputs(seed: int = 0) -> dict:
    key_of = jax.random.split(jax.random.key(seed), 8)
    inputs = heavy_noise(key_of[0], (TOKENS, D), 1.0, 24.0, ((0, 128),), (0, 1, 128, 5.5))
    grad_out = heavy_noise(key_of[1], (TOKENS, D), 1.0, 24.0, ((0, 128),), (0, 1, 128, 5.5))
    gate_pre = centred(key_of[2], (TOKENS, FF), 1.5, 6.0, ((0, 8), (1, 16)))
    up_pre = centred(key_of[3], (TOKENS, FF), 1.0, 6.0, ((0, 8), (1, 16)))
    w_gate = centred(key_of[4], (D, FF), D ** -0.5, 0.125, ((1, 16),))
    w_up = centred(key_of[5], (D, FF), D ** -0.5, 0.125, ((1, 16),))
    w_down = centred(key_of[6], (FF, D), FF ** -0.5, 0.078125, ((0, 16),))
    return {"inputs": inputs, "grad_out": grad_out, "gate_pre": gate_pre, "up_pre": up_pre, "w_gate": w_gate, "w_up": w_up, "w_down": w_down}


def reference(inputs, grad_out, gate_pre, up_pre, w_gate, w_up, w_down):
    gate = gate_pre.astype(jnp.float32)
    upper = up_pre.astype(jnp.float32)
    gate_sig = jax.nn.sigmoid(gate)
    gate_act = gate * gate_sig
    hidden = (gate_act * upper).astype(jnp.bfloat16)
    d_hidden = jnp.dot(grad_out, w_down.T, preferred_element_type=jnp.float32)
    d_gate = (d_hidden * upper * gate_sig * (1.0 + gate * (1.0 - gate_sig))).astype(jnp.bfloat16)
    d_up = (d_hidden * gate_act).astype(jnp.bfloat16)
    grad_down = jnp.dot(hidden.T, grad_out, preferred_element_type=jnp.float32)
    grad_gate = jnp.dot(inputs.T, d_gate, preferred_element_type=jnp.float32)
    grad_up = jnp.dot(inputs.T, d_up, preferred_element_type=jnp.float32)
    d_input = jnp.dot(d_gate, w_gate.T, preferred_element_type=jnp.float32)
    d_input = d_input + jnp.dot(d_up, w_up.T, preferred_element_type=jnp.float32)
    return (d_input, grad_gate, grad_up, grad_down)
```

```python
import jax
import jax.numpy as jnp
from jax import lax
from jax.sharding import PartitionSpec as P

NY, NX, NC = 2, 4, 2
NZ, NF = 4, 2


def tensor_pairs(move):
    index = lambda y, x, c: (y * NX + x) * NC + c
    return [(index(y, x, c), index(*move(y, x, c))) for y in range(NY) for x in range(NX) for c in range(NC)]


def dp_pairs(move):
    index = lambda z, f: z * NF + f
    return [(index(z, f), index(*move(z, f))) for z in range(NZ) for f in range(NF)]


CORE = tensor_pairs(lambda y, x, c: (y, x, 1 - c))
Y_SWAP = tensor_pairs(lambda y, x, c: (1 - y, x, c))
X_UP = tensor_pairs(lambda y, x, c: (y, (x + 1) % NX, c))
X_DOWN = tensor_pairs(lambda y, x, c: (y, (x - 1) % NX, c))
Z_UP = dp_pairs(lambda z, f: ((z + 1) % NZ, f))
Z_DOWN = dp_pairs(lambda z, f: ((z - 1) % NZ, f))
F_SWAP = dp_pairs(lambda z, f: (z, 1 - f))


def tsend(value, pairs):
    return lax.ppermute(value, "tensor", pairs)


def dsend(value, pairs):
    return lax.ppermute(value, "dp", pairs)


def gather_rows(own):
    half = own.shape[0] // 2
    other = tsend(own, Y_SWAP)
    rows = []
    for first in (own, other):
        below = tsend(first, X_UP)
        above = tsend(first, X_DOWN)
        far = [tsend(above[:half], X_DOWN), tsend(below[half:], X_UP)]
        rows += [first, above, *far, below]
    return jnp.concatenate(rows, axis=0)


def scatter_rows(partial):
    half = partial.shape[2] // 2
    low = lambda v: v.astype(jnp.bfloat16)
    up = tsend(low(partial[:, 2, :half]), X_UP)
    down = tsend(low(partial[:, 2, half:]), X_DOWN)
    above = jnp.concatenate([partial[:, 1, :half] + up, partial[:, 1, half:]], axis=1)
    below = jnp.concatenate([partial[:, 3, :half], partial[:, 3, half:] + down], axis=1)
    total = partial[:, 0] + tsend(low(above), X_UP) + tsend(low(below), X_DOWN)
    return total[0] + tsend(low(total[1]), Y_SWAP)


def sum_groups(both, z, f):
    low = lambda v: v.astype(jnp.bfloat16)
    features, width = both.shape[0], both.shape[1] // 2
    mine = both[:, :width] + tsend(low(both[:, width:]), CORE)
    mine = mine.reshape(NZ, NF, features // (NZ * NF), width)
    at = lambda d: lax.dynamic_index_in_dim(mine, (z + d) % NZ, 0, keepdims=False)
    far = low(at(2))
    up = dsend(far[0], Z_UP)
    down = dsend(far[1], Z_DOWN)
    one, three = at(1), at(3)
    above = jnp.stack([low(one[0] + up), low(one[1])])
    below = jnp.stack([low(three[0]), low(three[1] + down)])
    total = at(0) + dsend(above, Z_UP) + dsend(below, Z_DOWN)
    pick = lambda i: lax.dynamic_index_in_dim(total, i, 0, keepdims=False)
    return pick(f) + dsend(low(pick(1 - f)), F_SWAP)


def on_device(inputs, grad_out, gate_pre, up_pre, w_gate, w_up, w_down):
    place = lax.axis_index("tensor")
    c, x, y = place % NC, (place // NC) % NX, place // (NC * NX)
    group = lax.axis_index("dp")
    z, f = group // NF, group % NF
    rows = inputs.shape[0]

    def rows_of(value, core):
        blocks = [
            lax.dynamic_slice_in_dim(value, ((((y + dy) % NY) * NX + (x + dx) % NX) * NC + core) * rows, rows, 0)
            for dy in range(NY)
            for dx in range(NX)
        ]
        return jnp.concatenate(blocks, axis=0)

    cotangent = gather_rows(grad_out)
    down = jnp.concatenate([w_down, tsend(w_down, CORE)], axis=0)
    gate = jnp.concatenate([rows_of(gate_pre, c), tsend(rows_of(gate_pre, 1 - c), CORE)], axis=1).astype(jnp.float32)
    upper = jnp.concatenate([rows_of(up_pre, c), tsend(rows_of(up_pre, 1 - c), CORE)], axis=1).astype(jnp.float32)
    w_gate_all = jnp.concatenate([w_gate, tsend(w_gate, CORE)], axis=1)
    w_up_all = jnp.concatenate([w_up, tsend(w_up, CORE)], axis=1)

    gate_sig = jax.nn.sigmoid(gate)
    gate_act = gate * gate_sig
    hidden = (gate_act * upper).astype(jnp.bfloat16)
    d_hidden = jnp.einsum("rd,fd->rf", cotangent, down, preferred_element_type=jnp.float32)
    d_gate = (d_hidden * upper * gate_sig * (1.0 + gate * (1.0 - gate_sig))).astype(jnp.bfloat16)
    d_up = (d_hidden * gate_act).astype(jnp.bfloat16)

    rows_in = gather_rows(inputs)
    grad_down = jnp.einsum("rd,rf->df", cotangent, hidden, preferred_element_type=jnp.float32)
    down_part = sum_groups(grad_down, z, f).T
    term = jnp.einsum("rf,df->rd", d_gate, w_gate_all, preferred_element_type=jnp.float32)
    term = term + jnp.einsum("rf,df->rd", d_up, w_up_all, preferred_element_type=jnp.float32)
    d_input = scatter_rows(term.reshape(NY, NX, rows, -1))
    grad_gate = jnp.einsum("rd,rf->df", rows_in, d_gate, preferred_element_type=jnp.float32)
    gate_part = sum_groups(grad_gate, z, f)
    grad_up = jnp.einsum("rd,rf->df", rows_in, d_up, preferred_element_type=jnp.float32)
    up_part = sum_groups(grad_up, z, f)
    return (d_input, gate_part, up_part, down_part)


def solution(mesh):
    in_specs = (
        P(("dp", "tensor"), None),
        P(("dp", "tensor"), None),
        P("dp", "tensor"),
        P("dp", "tensor"),
        P(None, "tensor"),
        P(None, "tensor"),
        P("tensor", None),
    )
    out_specs = (P(("dp", "tensor"), None), P("dp", "tensor"), P("dp", "tensor"), P("tensor", "dp"))
    return jax.shard_map(
        on_device, mesh=mesh, in_specs=in_specs, out_specs=out_specs, check_vma=False
    )
```

```python
import jax
import jax.numpy as jnp
import numpy as np
from jax import lax
from jax.experimental import pallas as pl
from jax.experimental.pallas import tpu as pltpu
from jax.sharding import PartitionSpec as P

NY, NX, NC = 2, 4, 2
NZ, NF = 4, 2
BF, F32 = jnp.bfloat16, jnp.float32
ORDER = [(0, 0), (1, 0), (0, 1), (0, 3), (1, 1), (1, 3), (0, 2), (1, 2)]
CHUNKS = len(ORDER)
FARTHEST = (2, 1, 3, 0)


def tensor_pairs(move):
    index = lambda y, x, c: (y * NX + x) * NC + c
    return [(index(y, x, c), index(*move(y, x, c))) for y in range(NY) for x in range(NX) for c in range(NC)]


def dp_pairs(move):
    index = lambda z, f: z * NF + f
    return [(index(z, f), index(*move(z, f))) for z in range(NZ) for f in range(NF)]


CORE = tensor_pairs(lambda y, x, c: (y, x, 1 - c))
Y_SWAP = tensor_pairs(lambda y, x, c: (1 - y, x, c))
X_UP = tensor_pairs(lambda y, x, c: (y, (x + 1) % NX, c))
X_DOWN = tensor_pairs(lambda y, x, c: (y, (x - 1) % NX, c))
Z_UP = dp_pairs(lambda z, f: ((z + 1) % NZ, f))
Z_DOWN = dp_pairs(lambda z, f: ((z - 1) % NZ, f))
Z_FAR = dp_pairs(lambda z, f: ((z + 2) % NZ, f))
F_SWAP = dp_pairs(lambda z, f: (z, 1 - f))

ROWS = np.array(
    [
        [((y ^ dy) * NX + (x + dx) % NX) * NC + c for dy, dx in ORDER]
        for y in range(NY) for x in range(NX) for c in range(NC)
    ],
    np.int32,
)
SLABS = np.array(
    [
        [((z + dz) % NZ) * NF + (f ^ df) for dz in FARTHEST for df in range(NF)]
        for z in range(NZ) for f in range(NF)
    ],
    np.int32,
)
ANY = pl.BlockSpec(memory_space=pltpu.HBM)
VMEM = pl.BlockSpec(memory_space=pltpu.VMEM)
NT = (((1,), (1,)), ((), ()))
TN = (((0,), (0,)), ((), ()))


def tsend(value, pairs):
    return lax.ppermute(value, "tensor", pairs)


def dsend(value, pairs):
    return lax.ppermute(value, "dp", pairs)


def low(value):
    return value.astype(BF)


def params():
    return pltpu.CompilerParams(vmem_limit_bytes=60 << 20)


def cost(effort, flops, moved):
    return pl.CostEstimate(flops=int(flops * effort), bytes_accessed=int(moved * effort), transcendentals=0)


def hidden_body(table_ref, *refs):
    pre, (out,) = refs[:4], refs[4:]
    width = pre[0].shape[1]
    for core in range(NC):
        gate, upper = pre[core][...].astype(F32), pre[NC + core][...].astype(F32)
        out[:, core * width : (core + 1) * width] = (gate / (1.0 + jnp.exp(-gate)) * upper).astype(BF)


def hidden_call(table, pre, step, effort):
    width = pre[0].shape[1]
    total, both = step * CHUNKS, NC * width
    return pl.pallas_call(
        hidden_body,
        out_shape=jax.ShapeDtypeStruct((total, both), BF),
        grid_spec=pltpu.PrefetchScalarGridSpec(
            num_scalar_prefetch=1,
            grid=(CHUNKS,),
            in_specs=[pl.BlockSpec((step, width), lambda k, t: (t[k], 0))] * 4,
            out_specs=pl.BlockSpec((step, both), lambda k, t: (k, 0)),
        ),
        compiler_params=params(),
        cost_estimate=cost(effort, 16 * total * both, 6 * total * both),
        name="hidden",
    )(table, *pre)


def slope_body(first, count, table_ref, *refs):
    chunks, refs = refs[:count], refs[count:]
    down_pair, pre, (dgate_ref, dup_ref) = refs[:2], refs[2:6], refs[6:8]
    cot, down, gates, uppers, chunk_sem, down_sem, pre_sem = refs[8:]
    step = chunks[0].shape[0]
    width = pre[0].shape[1]

    def down_copy(j):
        return pltpu.make_async_copy(down_pair[j], down.at[pl.ds(j * width, width)], down_sem.at[j])

    def chunk_copy(k):
        return pltpu.make_async_copy(chunks[k], cot.at[pl.ds(k * step, step)], chunk_sem.at[k])

    def pre_copy(k, j):
        target = (gates, uppers)[j // 2]
        return pltpu.make_async_copy(
            pre[j].at[pl.ds(table_ref[first + k] * step, step)],
            target.at[pl.ds(k * step, step), pl.ds((j % 2) * width, width)],
            pre_sem.at[k, j],
        )

    for j in range(2):
        down_copy(j).start()
    for k in range(count):
        chunk_copy(k).start()
        for j in range(4):
            pre_copy(k, j).start()
    for j in range(2):
        down_copy(j).wait()
    tile = 2 * step
    for i in range(count // 2):
        for k in (2 * i, 2 * i + 1):
            chunk_copy(k).wait()
            for j in range(4):
                pre_copy(k, j).wait()
        at = pl.ds(i * tile, tile)
        d_hidden = lax.dot_general(cot[at, :], down[...], NT, preferred_element_type=F32)
        gate = gates[at, :].astype(F32)
        sig = 1.0 / (1.0 + jnp.exp(-gate))
        dgate_ref[at, :] = (d_hidden * uppers[at, :].astype(F32) * sig * (1.0 + gate * (1.0 - sig))).astype(BF)
        dup_ref[at, :] = (d_hidden * (gate * sig)).astype(BF)


def slope_call(table, first, chunks, downs, pre, effort):
    count = len(chunks)
    step, depth = chunks[0].shape
    width = downs[0].shape[0]
    total, both = step * count, NC * width
    out = jax.ShapeDtypeStruct((total, both), BF)
    return pl.pallas_call(
        lambda *refs: slope_body(first, count, *refs),
        out_shape=(out, out),
        grid_spec=pltpu.PrefetchScalarGridSpec(
            num_scalar_prefetch=1,
            grid=(1,),
            in_specs=[ANY] * (count + 6),
            out_specs=[pl.BlockSpec((total, both), lambda i, t: (0, 0))] * 2,
            scratch_shapes=[
                pltpu.VMEM((total, depth), BF),
                pltpu.VMEM((both, depth), BF),
                pltpu.VMEM((total, both), BF),
                pltpu.VMEM((total, both), BF),
                pltpu.SemaphoreType.DMA((count,)),
                pltpu.SemaphoreType.DMA((2,)),
                pltpu.SemaphoreType.DMA((count, 4)),
            ],
        ),
        compiler_params=params(),
        cost_estimate=cost(effort, 2 * total * depth * both, 8 << 20),
        name="slope",
    )(table, *chunks, *downs, *pre)


def weight_body(count, wide, table_ref, *refs):
    chunks, rights, (own_ref, other_ref) = refs[:count], refs[count:-2], refs[-2:]
    parts = len(rights) // wide
    step = chunks[0].shape[0]
    per = count // parts
    width = own_ref.shape[2] // wide
    for w in range(wide):
        both = None
        for p in range(parts):
            left = jnp.concatenate([c[...] for c in chunks[p * per : (p + 1) * per]], axis=0)
            term = lax.dot_general(left, rights[w * parts + p][...], TN, preferred_element_type=F32)
            both = term if both is None else both + term
        own_ref[0, :, w * width : (w + 1) * width] = both[:, :width]
        other_ref[0, :, w * width : (w + 1) * width] = both[:, width:].astype(BF)


def weight_call(table, first, slabs, sources, rights, effort):
    wide, parts = len(rights), len(rights[0])
    rows, both = rights[0][0].shape
    step, depth = rows * parts // CHUNKS, sources[0].shape[1]
    features = depth // (NZ * NF)
    slab = (slabs, features, wide * both // NC)
    at = lambda r, t: t[CHUNKS + first + r]
    if len(sources) == 1:
        chunks = sources * CHUNKS
        maps = [lambda r, t, k=k: (t[k], at(r, t)) for k in range(CHUNKS)]
    else:
        chunks = sources
        maps = [lambda r, t: (0, at(r, t))] * CHUNKS
    block = pl.BlockSpec((1, *slab[1:]), lambda r, t: (r, 0, 0))
    return pl.pallas_call(
        lambda *refs: weight_body(CHUNKS, wide, *refs),
        out_shape=(jax.ShapeDtypeStruct(slab, F32), jax.ShapeDtypeStruct(slab, BF)),
        grid_spec=pltpu.PrefetchScalarGridSpec(
            num_scalar_prefetch=1,
            grid=(slab[0],),
            in_specs=[pl.BlockSpec((step, features), m) for m in maps]
            + [pl.BlockSpec((rows, both), lambda r, t: (0, 0))] * (wide * parts),
            out_specs=[block, block],
        ),
        compiler_params=params(),
        cost_estimate=cost(effort, 2 * slabs * features * rows * parts * both * wide, 10 << 20),
        name="weight",
    )(table, *chunks, *[part for right in rights for part in right])


KEPT = [(0, 0), (1, 0), (1, 1), (0, 3)]


def input_body(parts, *refs):
    lefts, weights, outs = refs[: 2 * parts], refs[2 * parts : 2 * parts + 4], refs[2 * parts + 4 :]
    step = outs[0].shape[0]
    gate_weight = jnp.concatenate([weights[0][...], weights[1][...]], axis=1)
    up_weight = jnp.concatenate([weights[2][...], weights[3][...]], axis=1)
    per = CHUNKS // parts
    for p in range(parts):
        total = lax.dot_general(lefts[p][...], gate_weight, NT, preferred_element_type=F32)
        total = total + lax.dot_general(lefts[parts + p][...], up_weight, NT, preferred_element_type=F32)
        for k in range(per):
            out = outs[p * per + k]
            out[...] = total[k * step : (k + 1) * step].astype(out.dtype)


def input_call(d_gates, d_ups, weights, effort):
    depth, width = weights[0].shape
    parts = len(d_gates)
    rows, both = d_gates[0].shape
    step = rows * parts // CHUNKS
    tile = 256
    outs = pl.pallas_call(
        lambda *refs: input_body(parts, *refs),
        out_shape=[jax.ShapeDtypeStruct((step, depth), F32 if o in KEPT else BF) for o in ORDER],
        grid=(depth // tile,),
        in_specs=[pl.BlockSpec((rows, both), lambda n: (0, 0))] * (2 * parts)
        + [pl.BlockSpec((tile, width), lambda n: (n, 0))] * 4,
        out_specs=[pl.BlockSpec((step, tile), lambda n: (0, n))] * CHUNKS,
        compiler_params=params(),
        cost_estimate=cost(effort, 4 * rows * parts * depth * both, 14 << 20),
        name="input",
    )(*d_gates, *d_ups, *weights)
    return dict(zip(ORDER, outs))


def after(values, *events):
    return lax.optimization_barrier((values, events))[0]


def split(slabs):
    return slabs.reshape(-1, NF, *slabs.shape[1:])


def on_device(inputs, grad_out, gate_pre, up_pre, w_gate, w_up, w_down):
    table = jnp.concatenate([jnp.asarray(ROWS)[lax.axis_index("tensor")], jnp.asarray(SLABS)[lax.axis_index("dp")]])
    step, width = grad_out.shape[0], w_down.shape[0]
    half = CHUNKS // 2
    together = lambda *values: lax.optimization_barrier(values)

    other, above, below = tsend(grad_out, Y_SWAP), tsend(grad_out, X_DOWN), tsend(grad_out, X_UP)
    other, above, below, down_in, gate_in, inputs, up_pre = together(
        other, above, below, tsend(w_down, CORE), tsend(gate_pre, CORE), inputs, up_pre
    )
    near = [grad_out, other, above, below]
    above_y, below_y, far = tsend(other, X_DOWN), tsend(other, X_UP), tsend(above, X_DOWN)
    below_in, up_in = tsend(inputs, X_UP), tsend(up_pre, CORE)
    downs, pre = (w_down, down_in), (gate_pre, gate_in, up_pre, up_in)
    firsts = slope_call(table, 0, near, downs, pre, 4)
    hidden = hidden_call(table, pre, step, 1)

    above_y, below_y, far, below_in, inputs, w_gate, w_up, _, _ = together(
        above_y, below_y, far, below_in, inputs, w_gate, w_up, firsts[0], hidden
    )
    far_y = tsend(below_y, X_UP)
    above_in, other_in = tsend(inputs, X_DOWN), tsend(inputs, Y_SWAP)
    far_y, above_in, other_in, below_in, w_gate_in, w_up_in = together(
        far_y, above_in, other_in, below_in, tsend(w_gate, CORE), tsend(w_up, CORE)
    )
    last = [above_y, below_y, far, far_y]
    rows_in = [inputs, other_in, above_in, below_in]
    above_y, below_y = tsend(other_in, X_DOWN), tsend(other_in, X_UP)
    down_own, down_other = weight_call(table, 0, NZ * NF, near + last, [(hidden,)], 12)
    down_other = tsend(down_other, CORE)
    above_y, below_y, below_in, _ = together(above_y, below_y, below_in, down_own)
    seconds = slope_call(table, half, last, after(downs, above_y, below_y, down_own), pre, 12)
    far, far_y = tsend(below_in, X_UP), tsend(above_y, X_DOWN)
    rows_in += [above_y, below_y, far, far_y]
    d_gate, d_up = zip(firsts, seconds)
    partial = input_call(*after((d_gate, d_up), down_other), (w_gate, w_gate_in, w_up, w_up_in), 12)
    far_down, one_down, three_down, rest_down = split(down_own + down_other)
    far_down = dsend(low(far_down), Z_FAR)

    d_gate, d_up = after((d_gate, d_up), partial[0, 0], far_down)
    far_own, far_other = weight_call(table, 0, NF, rows_in, (d_gate, d_up), 0.1)
    far_other = tsend(far_other, CORE)
    one, three = tsend(after(partial[1, 2], far), X_UP), tsend(after(partial[1, 3], far_y), X_DOWN)
    one_down, three_down = after((low(one_down), low(three_down)), partial[0, 0])
    one_down, three_down = dsend(one_down, Z_UP), dsend(three_down, Z_DOWN)
    d_gate, d_up, one, three, one_down, three_down, below = together(d_gate, d_up, one, three, one_down, three_down, partial[0, 2])
    d_gate, d_up = after((d_gate, d_up), far_own, far_other)
    rest_own, rest_other = weight_call(table, NF, NZ * NF - NF, rows_in, (d_gate, d_up), 12)
    far_sum = low(far_own + far_other)
    far_up, far_dn = dsend(far_sum[0], Z_UP), dsend(far_sum[1], Z_DOWN)
    above, below = tsend(low(partial[1, 1] + one), X_UP), tsend(below, X_DOWN)
    far_up, far_dn, rest_other, above, below, up = together(far_up, far_dn, rest_other, above, below, partial[0, 1])
    rest_one, rest_three, rest = split(rest_own + tsend(rest_other, CORE))
    rest_up = dsend(jnp.stack([low(rest_one[0] + far_up), low(rest_one[1])]), Z_UP)
    rest_dn = dsend(jnp.stack([low(rest_three[0]), low(rest_three[1] + far_dn)]), Z_DOWN)
    total = tsend(low(partial[1, 0] + above + three), Y_SWAP)
    below, up = tsend(low(partial[0, 3] + below), X_DOWN), tsend(up, X_UP)
    rest_up, rest_dn, below, up = together(rest_up, rest_dn, below, up)
    d_input = partial[0, 0] + below + up + total
    rest = rest + rest_up + rest_dn
    rest_down = rest_down + one_down + three_down + far_down
    down_part = (rest_down[0] + dsend(low(rest_down[1]), F_SWAP)).T
    both_part = rest[0] + dsend(low(rest[1]), F_SWAP)
    return (d_input, both_part[:, :width], both_part[:, width:], down_part)


def solution(mesh):
    in_specs = (
        P(("dp", "tensor"), None),
        P(("dp", "tensor"), None),
        P("dp", "tensor"),
        P("dp", "tensor"),
        P(None, "tensor"),
        P(None, "tensor"),
        P("tensor", None),
    )
    out_specs = (P(("dp", "tensor"), None), P("dp", "tensor"), P("dp", "tensor"), P("tensor", "dp"))
    return jax.shard_map(
        on_device, mesh=mesh, in_specs=in_specs, out_specs=out_specs, check_vma=False
    )
```

```python
import jax
import jax.numpy as jnp
import numpy as np
from jax import lax
from jax.experimental import pallas as pl
from jax.experimental.pallas import tpu as pltpu
from jax.sharding import PartitionSpec as P

NY, NX, NC = 2, 4, 2
NZ, NF = 4, 2
BF, F32 = jnp.bfloat16, jnp.float32
ORDER = [(0, 0), (1, 0), (0, 1), (0, 3), (1, 1), (1, 3), (0, 2), (1, 2)]
CHUNKS = len(ORDER)


def tensor_pairs(move):
    index = lambda y, x, c: (y * NX + x) * NC + c
    return [(index(y, x, c), index(*move(y, x, c))) for y in range(NY) for x in range(NX) for c in range(NC)]


def dp_pairs(move):
    index = lambda z, f: z * NF + f
    return [(index(z, f), index(*move(z, f))) for z in range(NZ) for f in range(NF)]


CORE = tensor_pairs(lambda y, x, c: (y, x, 1 - c))
Y_SWAP = tensor_pairs(lambda y, x, c: (1 - y, x, c))
X_UP = tensor_pairs(lambda y, x, c: (y, (x + 1) % NX, c))
X_DOWN = tensor_pairs(lambda y, x, c: (y, (x - 1) % NX, c))
Z_UP = dp_pairs(lambda z, f: ((z + 1) % NZ, f))
Z_DOWN = dp_pairs(lambda z, f: ((z - 1) % NZ, f))
Z_FAR = dp_pairs(lambda z, f: ((z + 2) % NZ, f))
F_SWAP = dp_pairs(lambda z, f: (z, 1 - f))

FARTHEST = (2, 1, 3, 0)
ROWS = np.array(
    [
        [((y ^ dy) * NX + (x + dx) % NX) * NC + c for dy, dx in ORDER]
        for y in range(NY) for x in range(NX) for c in range(NC)
    ],
    np.int32,
)
SLABS = np.array([[*((z + dz) % NZ for dz in FARTHEST), f] for z in range(NZ) for f in range(NF)], np.int32)
ANY = pl.BlockSpec(memory_space=pltpu.HBM)
VMEM = pl.BlockSpec(memory_space=pltpu.VMEM)
NT = (((1,), (1,)), ((), ()))
TN = (((0,), (0,)), ((), ()))


def tsend(value, pairs):
    return lax.ppermute(value, "tensor", pairs)


def dsend(value, pairs):
    return lax.ppermute(value, "dp", pairs)


def low(value):
    return value.astype(BF)


def params():
    return pltpu.CompilerParams(vmem_limit_bytes=24 << 20)


def cost(effort, flops, moved):
    return pl.CostEstimate(flops=int(flops * effort), bytes_accessed=int(moved * effort), transcendentals=0)


def hidden_body(table_ref, *refs):
    pre, (out,) = refs[:4], refs[4:]
    width = pre[0].shape[1]
    for core in range(NC):
        gate, upper = pre[core][...].astype(F32), pre[NC + core][...].astype(F32)
        out[:, core * width : (core + 1) * width] = (gate / (1.0 + jnp.exp(-gate)) * upper).astype(BF)


def hidden_call(table, pre, step, effort):
    width = pre[0].shape[1]
    total, both = step * CHUNKS, NC * width
    return pl.pallas_call(
        hidden_body,
        out_shape=jax.ShapeDtypeStruct((total, both), BF),
        grid_spec=pltpu.PrefetchScalarGridSpec(
            num_scalar_prefetch=1,
            grid=(CHUNKS,),
            in_specs=[pl.BlockSpec((step, width), lambda k, t: (t[k], 0))] * 4,
            out_specs=pl.BlockSpec((step, both), lambda k, t: (k, 0)),
        ),
        compiler_params=params(),
        cost_estimate=cost(effort, 16 * total * both, 6 * total * both),
        name="hidden",
    )(table, *pre)


def slope_body(first, count, table_ref, *refs):
    chunks, refs = refs[:count], refs[count:]
    down_pair, pre, (dgate_ref, dup_ref) = refs[:2], refs[2:6], refs[6:8]
    cot, down, gates, uppers, chunk_sem, down_sem, pre_sem = refs[8:]
    step = cot.shape[0] // (CHUNKS // 2)
    width = pre[0].shape[1]
    starts = np.cumsum([0] + [c.shape[0] for c in chunks]).tolist()

    def down_copy(j):
        return pltpu.make_async_copy(down_pair[j], down.at[pl.ds(j * width, width)], down_sem.at[j])

    def chunk_copy(k):
        return pltpu.make_async_copy(chunks[k], cot.at[pl.ds(starts[k], chunks[k].shape[0])], chunk_sem.at[k])

    def pre_copy(k, j):
        target = (gates, uppers)[j // 2]
        return pltpu.make_async_copy(
            pre[j].at[pl.ds(table_ref[first + k] * step, step)],
            target.at[pl.ds(k * step, step), pl.ds((j % 2) * width, width)],
            pre_sem.at[k, j],
        )

    for j in range(2):
        down_copy(j).start()
    for k in range(count):
        chunk_copy(k).start()
    for k in range(CHUNKS // 2):
        for j in range(4):
            pre_copy(k, j).start()
    for j in range(2):
        down_copy(j).wait()
    tile = 2 * step
    for i in range(CHUNKS // 4):
        for k in range(count):
            if i * tile <= starts[k] < (i + 1) * tile:
                chunk_copy(k).wait()
        for k in (2 * i, 2 * i + 1):
            for j in range(4):
                pre_copy(k, j).wait()
        at = pl.ds(i * tile, tile)
        d_hidden = lax.dot_general(cot[at, :], down[...], NT, preferred_element_type=F32)
        gate = gates[at, :].astype(F32)
        sig = 1.0 / (1.0 + jnp.exp(-gate))
        dgate_ref[at, :] = (d_hidden * uppers[at, :].astype(F32) * sig * (1.0 + gate * (1.0 - sig))).astype(BF)
        dup_ref[at, :] = (d_hidden * (gate * sig)).astype(BF)


def slope_call(table, first, chunks, downs, pre, effort):
    count = len(chunks)
    total, depth = sum(c.shape[0] for c in chunks), chunks[0].shape[1]
    width = downs[0].shape[0]
    both = NC * width
    out = jax.ShapeDtypeStruct((total, both), BF)
    return pl.pallas_call(
        lambda *refs: slope_body(first, count, *refs),
        out_shape=(out, out),
        grid_spec=pltpu.PrefetchScalarGridSpec(
            num_scalar_prefetch=1,
            grid=(1,),
            in_specs=[ANY] * (count + 6),
            out_specs=[pl.BlockSpec((total, both), lambda i, t: (0, 0))] * 2,
            scratch_shapes=[
                pltpu.VMEM((total, depth), BF),
                pltpu.VMEM((both, depth), BF),
                pltpu.VMEM((total, both), BF),
                pltpu.VMEM((total, both), BF),
                pltpu.SemaphoreType.DMA((count,)),
                pltpu.SemaphoreType.DMA((2,)),
                pltpu.SemaphoreType.DMA((CHUNKS // 2, 4)),
            ],
        ),
        compiler_params=params(),
        cost_estimate=cost(effort, 2 * total * depth * both, 8 << 20),
        name="slope",
    )(table, *chunks, *downs, *pre)


def weight_body(count, wide, table_ref, *refs):
    chunks, rights, (own_ref, other_ref) = refs[:count], refs[count:-2], refs[-2:]
    parts = len(rights) // wide
    features = own_ref.shape[1]
    width = own_ref.shape[2] // wide
    far = table_ref[CHUNKS + NZ]
    starts = np.cumsum([0] + [c.shape[0] for c in chunks]).tolist()
    per = starts[-1] // parts
    lefts = [
        jnp.concatenate([c[...] for c, start in zip(chunks, starts) if p * per <= start < (p + 1) * per], axis=0)
        for p in range(parts)
    ]
    for w in range(wide):
        both = None
        for p in range(parts):
            term = lax.dot_general(lefts[p], rights[w * parts + p][...], TN, preferred_element_type=F32)
            both = term if both is None else both + term
        at = pl.ds(w * width, width)
        for f in range(NF):
            slab = both[f * features : (f + 1) * features]
            own_ref[f ^ far, :, at] = slab[:, :width]
            other_ref[f ^ far, :, at] = slab[:, width:].astype(BF)


def weight_call(table, first, blocks, chunks, rights, effort):
    count, wide, parts = len(chunks), len(rights), len(rights[0])
    rows, both = rights[0][0].shape
    depth = chunks[0].shape[1]
    features = depth // (NZ * NF)
    slab = (blocks * NF, features, wide * both // NC)
    block = pl.BlockSpec((NF, *slab[1:]), lambda r, t: (r, 0, 0))
    return pl.pallas_call(
        lambda *refs: weight_body(count, wide, *refs),
        out_shape=(jax.ShapeDtypeStruct(slab, F32), jax.ShapeDtypeStruct(slab, BF)),
        grid_spec=pltpu.PrefetchScalarGridSpec(
            num_scalar_prefetch=1,
            grid=(blocks,),
            in_specs=[pl.BlockSpec((c.shape[0], NF * features), lambda r, t: (0, t[CHUNKS + first + r])) for c in chunks]
            + [pl.BlockSpec((rows, both), lambda r, t: (0, 0))] * (wide * parts),
            out_specs=[block, block],
        ),
        compiler_params=params(),
        cost_estimate=cost(effort, 2 * blocks * NF * features * rows * parts * both * wide, 10 << 20),
        name="weight",
    )(table, *chunks, *[part for right in rights for part in right])


def ring_body(own_up, own_down, in_up, in_down, far_up, far_down, up_ref, down_ref):
    up = own_up[...] + in_up[...].astype(F32)
    down = own_down[...] + in_down[...].astype(F32)

    @pl.when(pl.program_id(0) == 0)
    def _():
        up_ref[...] = (up + far_up[...].astype(F32)).astype(BF)
        down_ref[...] = down.astype(BF)

    @pl.when(pl.program_id(0) == 1)
    def _():
        up_ref[...] = up.astype(BF)
        down_ref[...] = (down + far_down[...].astype(F32)).astype(BF)


def ring_call(own, other, far_up, far_down):
    _, features, width = own.shape
    first = pl.BlockSpec((1, features, width), lambda f: (f, 0, 0))
    second = pl.BlockSpec((1, features, width), lambda f: (NF + f, 0, 0))
    whole = pl.BlockSpec((1, features, width), lambda f: (0, 0, 0))
    out = jax.ShapeDtypeStruct((NF, features, width), BF)
    return pl.pallas_call(
        ring_body,
        out_shape=(out, out),
        grid=(NF,),
        in_specs=[first, second, first, second, whole, whole],
        out_specs=[first, first],
        compiler_params=params(),
        cost_estimate=cost(1, 8 * own.size, 8 * own.size),
        name="ring",
    )(own, own, other, other, far_up[None], far_down[None])


KEPT = [(0, 0), (1, 0), (1, 1), (0, 3)]


def input_body(parts, *refs):
    lefts, weights, outs = refs[: 2 * parts], refs[2 * parts : 2 * parts + 4], refs[2 * parts + 4 :]
    step = outs[0].shape[0]
    gate_weight = jnp.concatenate([weights[0][...], weights[1][...]], axis=1)
    up_weight = jnp.concatenate([weights[2][...], weights[3][...]], axis=1)
    per = CHUNKS // parts
    for p in range(parts):
        total = lax.dot_general(lefts[p][...], gate_weight, NT, preferred_element_type=F32)
        total = total + lax.dot_general(lefts[parts + p][...], up_weight, NT, preferred_element_type=F32)
        for k in range(per):
            out = outs[p * per + k]
            out[...] = total[k * step : (k + 1) * step].astype(out.dtype)


def input_call(d_gates, d_ups, weights, effort):
    depth, width = weights[0].shape
    parts = len(d_gates)
    rows, both = d_gates[0].shape
    step = rows * parts // CHUNKS
    tile = 512
    outs = pl.pallas_call(
        lambda *refs: input_body(parts, *refs),
        out_shape=[jax.ShapeDtypeStruct((step, depth), F32 if o in KEPT else BF) for o in ORDER],
        grid=(depth // tile,),
        in_specs=[pl.BlockSpec((rows, both), lambda n: (0, 0))] * (2 * parts)
        + [pl.BlockSpec((tile, width), lambda n: (n, 0))] * 4,
        out_specs=[pl.BlockSpec((step, tile), lambda n: (0, n))] * CHUNKS,
        compiler_params=params(),
        cost_estimate=cost(effort, 4 * rows * parts * depth * both, 14 << 20),
        name="input",
    )(*d_gates, *d_ups, *weights)
    return dict(zip(ORDER, outs))


def after(values, *events):
    return lax.optimization_barrier((values, events))[0]


def split(slabs):
    return slabs.reshape(-1, NF, *slabs.shape[1:])


def on_device(inputs, grad_out, gate_pre, up_pre, w_gate, w_up, w_down):
    table = jnp.concatenate([jnp.asarray(ROWS)[lax.axis_index("tensor")], jnp.asarray(SLABS)[lax.axis_index("dp")]])
    step, width = grad_out.shape[0], w_down.shape[0]
    part = step // 2
    together = lambda *values: lax.optimization_barrier(values)

    other, above, below = tsend(grad_out, Y_SWAP), tsend(grad_out, X_DOWN), tsend(grad_out, X_UP)
    other, above, below, down_in, gate_in, up_pre = together(
        other, above, below, tsend(w_down, CORE), tsend(gate_pre, CORE), up_pre
    )
    near = [grad_out, other, above, below]
    above_y, below_y = tsend(other, X_DOWN), tsend(other, X_UP)
    far = [tsend(above[:part], X_DOWN), tsend(below[part:], X_UP)]
    up_in = tsend(up_pre, CORE)
    downs, pre = (w_down, down_in), (gate_pre, gate_in, up_pre, up_in)
    firsts = slope_call(table, 0, near, downs, pre, 4)
    hidden = hidden_call(table, pre, step, 1)

    above_y, below_y, far, inputs, w_gate, w_up, _, _ = together(
        above_y, below_y, far, inputs, w_gate, w_up, firsts[0], hidden
    )
    far_y = [tsend(above_y[:part], X_DOWN), tsend(below_y[part:], X_UP)]
    far_y, other_in, w_gate_in, w_up_in, inputs = together(
        far_y, tsend(inputs, Y_SWAP), tsend(w_gate, CORE), tsend(w_up, CORE), inputs
    )
    last = [above_y, below_y, *far, *far_y]

    above_in, below_in = tsend(inputs, X_DOWN), tsend(inputs, X_UP)
    down_own, down_other = weight_call(table, 0, NZ, near + last, [(hidden,)], 12)
    down_other = tsend(down_other, CORE)
    above_in, below_in, other_in, _ = together(above_in, below_in, other_in, down_own)
    rows_in = [inputs, other_in, above_in, below_in]
    above_y, below_y = tsend(other_in, X_DOWN), tsend(other_in, X_UP)
    seconds = slope_call(table, CHUNKS // 2, last, after(downs, above_in, below_in, down_own), pre, 12)
    above_y, below_y, below_in = together(above_y, below_y, below_in)
    far, far_y = tsend(below_in, X_UP), tsend(above_y, X_DOWN)
    rows_in += [above_y, below_y, far, far_y]
    d_gate, d_up = zip(firsts, seconds)
    partial = input_call(*after((d_gate, d_up), down_other, above_y, below_y), (w_gate, w_gate_in, w_up, w_up_in), 12)
    far_down, one_down, three_down, rest_down = split(down_own + down_other)
    far_down = dsend(low(far_down), Z_FAR)

    d_gate, d_up = after((d_gate, d_up), partial[0, 0], far_down)
    far_own, far_other = weight_call(table, 0, 1, rows_in, (d_gate, d_up), 0.1)
    far_other = tsend(far_other, CORE)
    one, three = tsend(after(partial[1, 2], far), X_UP), tsend(after(partial[1, 3], far_y), X_DOWN)
    one_down, three_down = after((low(one_down), low(three_down)), partial[0, 0])
    one_down, three_down = dsend(one_down, Z_UP), dsend(three_down, Z_DOWN)
    d_gate, d_up, one, three, one_down, three_down, below = together(
        d_gate, d_up, one, three, one_down, three_down, partial[0, 2]
    )
    d_gate, d_up = after((d_gate, d_up), far_own, far_other)
    ring_own, ring_other = weight_call(table, 1, 2, rows_in, (d_gate, d_up), 12)
    far_sum = low(far_own + far_other)
    far_up, far_dn = dsend(far_sum[0], Z_UP), dsend(far_sum[1], Z_DOWN)
    above, below = tsend(low(partial[1, 1] + one), X_UP), tsend(below, X_DOWN)
    far_up, far_dn, ring_other, above, below, up = together(far_up, far_dn, ring_other, above, below, partial[0, 1])
    d_gate, d_up = after((d_gate, d_up), ring_own)
    rest_own, rest_other = weight_call(table, 3, 1, rows_in, (d_gate, d_up), 12)
    ring_up, ring_dn = ring_call(ring_own, tsend(ring_other, CORE), *after((far_up, far_dn), rest_own))
    rest_other = tsend(rest_other, CORE)
    ring_up, ring_dn = dsend(ring_up, Z_UP), dsend(ring_dn, Z_DOWN)
    total = tsend(low(after(partial[1, 0], rest_other) + above + three), Y_SWAP)
    below, up = tsend(low(partial[0, 3] + below), X_DOWN), tsend(up, X_UP)
    ring_up, ring_dn, below, up, rest_down = together(ring_up, ring_dn, below, up, rest_down)
    rest_down = rest_down + one_down + three_down + far_down
    rest = rest_own + rest_other + ring_up + ring_dn
    d_input = partial[0, 0] + below + up + total
    down_part = (rest_down[0] + dsend(low(rest_down[1]), F_SWAP)).T
    both_part = rest[0] + dsend(low(rest[1]), F_SWAP)
    return (d_input, both_part[:, :width], both_part[:, width:], down_part)


def solution(mesh):
    in_specs = (
        P(("dp", "tensor"), None),
        P(("dp", "tensor"), None),
        P("dp", "tensor"),
        P("dp", "tensor"),
        P(None, "tensor"),
        P(None, "tensor"),
        P("tensor", None),
    )
    out_specs = (P(("dp", "tensor"), None), P("dp", "tensor"), P("dp", "tensor"), P("tensor", "dp"))
    return jax.shard_map(
        on_device, mesh=mesh, in_specs=in_specs, out_specs=out_specs, check_vma=False
    )
```

```python
import jax
import jax.numpy as jnp
import numpy as np
from jax import lax
from jax.experimental import pallas as pl
from jax.experimental.pallas import tpu as pltpu
from jax.sharding import PartitionSpec as P

NY, NX, NC = 2, 4, 2
NZ, NF = 4, 2
BF, F32 = jnp.bfloat16, jnp.float32
ORDER = [(0, 0), (1, 0), (0, 1), (0, 3), (1, 1), (1, 3), (0, 2), (1, 2)]
CHUNKS = len(ORDER)


def tensor_pairs(move):
    index = lambda y, x, c: (y * NX + x) * NC + c
    return [(index(y, x, c), index(*move(y, x, c))) for y in range(NY) for x in range(NX) for c in range(NC)]


def dp_pairs(move):
    index = lambda z, f: z * NF + f
    return [(index(z, f), index(*move(z, f))) for z in range(NZ) for f in range(NF)]


CORE = tensor_pairs(lambda y, x, c: (y, x, 1 - c))
Y_SWAP = tensor_pairs(lambda y, x, c: (1 - y, x, c))
X_UP = tensor_pairs(lambda y, x, c: (y, (x + 1) % NX, c))
X_DOWN = tensor_pairs(lambda y, x, c: (y, (x - 1) % NX, c))
Z_UP = dp_pairs(lambda z, f: ((z + 1) % NZ, f))
Z_DOWN = dp_pairs(lambda z, f: ((z - 1) % NZ, f))
Z_FAR = dp_pairs(lambda z, f: ((z + 2) % NZ, f))
F_SWAP = dp_pairs(lambda z, f: (z, 1 - f))

FARTHEST = (2, 1, 3, 0)
ROWS = np.array(
    [
        [((y ^ dy) * NX + (x + dx) % NX) * NC + c for dy, dx in ORDER]
        for y in range(NY) for x in range(NX) for c in range(NC)
    ],
    np.int32,
)
SLABS = np.array([[*((z + dz) % NZ for dz in FARTHEST), f] for z in range(NZ) for f in range(NF)], np.int32)
ANY = pl.BlockSpec(memory_space=pltpu.HBM)
VMEM = pl.BlockSpec(memory_space=pltpu.VMEM)
NT = (((1,), (1,)), ((), ()))
TN = (((0,), (0,)), ((), ()))


def tsend(value, pairs):
    return lax.ppermute(value, "tensor", pairs)


def dsend(value, pairs):
    return lax.ppermute(value, "dp", pairs)


def low(value):
    return value.astype(BF)


def params():
    return pltpu.CompilerParams(vmem_limit_bytes=24 << 20)


def cost(effort, flops, moved):
    return pl.CostEstimate(flops=int(flops * effort), bytes_accessed=int(moved * effort), transcendentals=0)


def hidden_body(table_ref, *refs):
    pre, (out,) = refs[:4], refs[4:]
    width = pre[0].shape[1]
    for core in range(NC):
        gate, upper = pre[core][...].astype(F32), pre[NC + core][...].astype(F32)
        out[:, core * width : (core + 1) * width] = (gate / (1.0 + jnp.exp(-gate)) * upper).astype(BF)


def hidden_call(table, pre, step, effort):
    width = pre[0].shape[1]
    total, both = step * CHUNKS, NC * width
    return pl.pallas_call(
        hidden_body,
        out_shape=jax.ShapeDtypeStruct((total, both), BF),
        grid_spec=pltpu.PrefetchScalarGridSpec(
            num_scalar_prefetch=1,
            grid=(CHUNKS,),
            in_specs=[pl.BlockSpec((step, width), lambda k, t: (t[k], 0))] * 4,
            out_specs=pl.BlockSpec((step, both), lambda k, t: (k, 0)),
        ),
        compiler_params=params(),
        cost_estimate=cost(effort, 16 * total * both, 6 * total * both),
        name="hidden",
    )(table, *pre)


def slope_body(first, count, table_ref, *refs):
    chunks, refs = refs[:count], refs[count:]
    down_pair, pre, (dgate_ref, dup_ref) = refs[:2], refs[2:6], refs[6:8]
    cot, down, gates, uppers, chunk_sem, down_sem, pre_sem = refs[8:]
    step = cot.shape[0] // (CHUNKS // 2)
    width = pre[0].shape[1]
    starts = np.cumsum([0] + [c.shape[0] for c in chunks]).tolist()

    def down_copy(j):
        return pltpu.make_async_copy(down_pair[j], down.at[pl.ds(j * width, width)], down_sem.at[j])

    def chunk_copy(k):
        return pltpu.make_async_copy(chunks[k], cot.at[pl.ds(starts[k], chunks[k].shape[0])], chunk_sem.at[k])

    def pre_copy(k, j):
        target = (gates, uppers)[j // 2]
        return pltpu.make_async_copy(
            pre[j].at[pl.ds(table_ref[first + k] * step, step)],
            target.at[pl.ds(k * step, step), pl.ds((j % 2) * width, width)],
            pre_sem.at[k, j],
        )

    for j in range(2):
        down_copy(j).start()
    for k in range(count):
        chunk_copy(k).start()
    for k in range(CHUNKS // 2):
        for j in range(4):
            pre_copy(k, j).start()
    for j in range(2):
        down_copy(j).wait()
    tile = 2 * step
    for i in range(CHUNKS // 4):
        for k in range(count):
            if i * tile <= starts[k] < (i + 1) * tile:
                chunk_copy(k).wait()
        for k in (2 * i, 2 * i + 1):
            for j in range(4):
                pre_copy(k, j).wait()
        at = pl.ds(i * tile, tile)
        d_hidden = lax.dot_general(cot[at, :], down[...], NT, preferred_element_type=F32)
        gate = gates[at, :].astype(F32)
        sig = 1.0 / (1.0 + jnp.exp(-gate))
        dgate_ref[at, :] = (d_hidden * uppers[at, :].astype(F32) * sig * (1.0 + gate * (1.0 - sig))).astype(BF)
        dup_ref[at, :] = (d_hidden * (gate * sig)).astype(BF)


def slope_call(table, first, chunks, downs, pre, effort):
    count = len(chunks)
    total, depth = sum(c.shape[0] for c in chunks), chunks[0].shape[1]
    width = downs[0].shape[0]
    both = NC * width
    out = jax.ShapeDtypeStruct((total, both), BF)
    return pl.pallas_call(
        lambda *refs: slope_body(first, count, *refs),
        out_shape=(out, out),
        grid_spec=pltpu.PrefetchScalarGridSpec(
            num_scalar_prefetch=1,
            grid=(1,),
            in_specs=[ANY] * (count + 6),
            out_specs=[pl.BlockSpec((total, both), lambda i, t: (0, 0))] * 2,
            scratch_shapes=[
                pltpu.VMEM((total, depth), BF),
                pltpu.VMEM((both, depth), BF),
                pltpu.VMEM((total, both), BF),
                pltpu.VMEM((total, both), BF),
                pltpu.SemaphoreType.DMA((count,)),
                pltpu.SemaphoreType.DMA((2,)),
                pltpu.SemaphoreType.DMA((CHUNKS // 2, 4)),
            ],
        ),
        compiler_params=params(),
        cost_estimate=cost(effort, 2 * total * depth * both, 8 << 20),
        name="slope",
    )(table, *chunks, *downs, *pre)


def weight_body(count, wide, table_ref, *refs):
    chunks, rights, (own_ref, other_ref) = refs[:count], refs[count:-2], refs[-2:]
    parts = len(rights) // wide
    features = own_ref.shape[1]
    width = own_ref.shape[2] // wide
    far = table_ref[CHUNKS + NZ]
    starts = np.cumsum([0] + [c.shape[0] for c in chunks]).tolist()
    per = starts[-1] // parts
    lefts = [
        jnp.concatenate([c[...] for c, start in zip(chunks, starts) if p * per <= start < (p + 1) * per], axis=0)
        for p in range(parts)
    ]
    for w in range(wide):
        both = None
        for p in range(parts):
            term = lax.dot_general(lefts[p], rights[w * parts + p][...], TN, preferred_element_type=F32)
            both = term if both is None else both + term
        at = pl.ds(w * width, width)
        for f in range(NF):
            slab = both[f * features : (f + 1) * features]
            own_ref[f ^ far, :, at] = slab[:, :width]
            other_ref[f ^ far, :, at] = slab[:, width:].astype(BF)


def weight_call(table, first, blocks, chunks, rights, effort):
    count, wide, parts = len(chunks), len(rights), len(rights[0])
    rows, both = rights[0][0].shape
    depth = chunks[0].shape[1]
    features = depth // (NZ * NF)
    slab = (blocks * NF, features, wide * both // NC)
    block = pl.BlockSpec((NF, *slab[1:]), lambda r, t: (r, 0, 0))
    return pl.pallas_call(
        lambda *refs: weight_body(count, wide, *refs),
        out_shape=(jax.ShapeDtypeStruct(slab, F32), jax.ShapeDtypeStruct(slab, BF)),
        grid_spec=pltpu.PrefetchScalarGridSpec(
            num_scalar_prefetch=1,
            grid=(blocks,),
            in_specs=[pl.BlockSpec((c.shape[0], NF * features), lambda r, t: (0, t[CHUNKS + first + r])) for c in chunks]
            + [pl.BlockSpec((rows, both), lambda r, t: (0, 0))] * (wide * parts),
            out_specs=[block, block],
        ),
        compiler_params=params(),
        cost_estimate=cost(effort, 2 * blocks * NF * features * rows * parts * both * wide, 10 << 20),
        name="weight",
    )(table, *chunks, *[part for right in rights for part in right])


def ring_body(own_up, own_down, in_up, in_down, far_up, far_down, up_ref, down_ref):
    up = own_up[...] + in_up[...].astype(F32)
    down = own_down[...] + in_down[...].astype(F32)

    @pl.when(pl.program_id(0) == 0)
    def _():
        up_ref[...] = (up + far_up[...].astype(F32)).astype(BF)
        down_ref[...] = down.astype(BF)

    @pl.when(pl.program_id(0) == 1)
    def _():
        up_ref[...] = up.astype(BF)
        down_ref[...] = (down + far_down[...].astype(F32)).astype(BF)


def ring_call(own, other, far_up, far_down):
    _, features, width = own.shape
    first = pl.BlockSpec((1, features, width), lambda f: (f, 0, 0))
    second = pl.BlockSpec((1, features, width), lambda f: (NF + f, 0, 0))
    whole = pl.BlockSpec((1, features, width), lambda f: (0, 0, 0))
    out = jax.ShapeDtypeStruct((NF, features, width), BF)
    return pl.pallas_call(
        ring_body,
        out_shape=(out, out),
        grid=(NF,),
        in_specs=[first, second, first, second, whole, whole],
        out_specs=[first, first],
        compiler_params=params(),
        cost_estimate=cost(1, 8 * own.size, 8 * own.size),
        name="ring",
    )(own, own, other, other, far_up[None], far_down[None])


KEPT = [(0, 0), (1, 0), (1, 1), (0, 3)]


def input_body(parts, *refs):
    lefts, weights, outs = refs[: 2 * parts], refs[2 * parts : 2 * parts + 4], refs[2 * parts + 4 :]
    step = outs[0].shape[0]
    gate_weight = jnp.concatenate([weights[0][...], weights[1][...]], axis=1)
    up_weight = jnp.concatenate([weights[2][...], weights[3][...]], axis=1)
    per = CHUNKS // parts
    for p in range(parts):
        total = lax.dot_general(lefts[p][...], gate_weight, NT, preferred_element_type=F32)
        total = total + lax.dot_general(lefts[parts + p][...], up_weight, NT, preferred_element_type=F32)
        for k in range(per):
            out = outs[p * per + k]
            out[...] = total[k * step : (k + 1) * step].astype(out.dtype)


def input_call(d_gates, d_ups, weights, effort):
    depth, width = weights[0].shape
    parts = len(d_gates)
    rows, both = d_gates[0].shape
    step = rows * parts // CHUNKS
    tile = 512
    outs = pl.pallas_call(
        lambda *refs: input_body(parts, *refs),
        out_shape=[jax.ShapeDtypeStruct((step, depth), F32 if o in KEPT else BF) for o in ORDER],
        grid=(depth // tile,),
        in_specs=[pl.BlockSpec((rows, both), lambda n: (0, 0))] * (2 * parts)
        + [pl.BlockSpec((tile, width), lambda n: (n, 0))] * 4,
        out_specs=[pl.BlockSpec((step, tile), lambda n: (0, n))] * CHUNKS,
        compiler_params=params(),
        cost_estimate=cost(effort, 4 * rows * parts * depth * both, 14 << 20),
        name="input",
    )(*d_gates, *d_ups, *weights)
    return dict(zip(ORDER, outs))


def after(values, *events):
    return lax.optimization_barrier((values, events))[0]


def split(slabs):
    return slabs.reshape(-1, NF, *slabs.shape[1:])


def on_device(inputs, grad_out, gate_pre, up_pre, w_gate, w_up, w_down):
    table = jnp.concatenate([jnp.asarray(ROWS)[lax.axis_index("tensor")], jnp.asarray(SLABS)[lax.axis_index("dp")]])
    step, width = grad_out.shape[0], w_down.shape[0]
    part = step // 2
    together = lambda *values: lax.optimization_barrier(values)

    other, above, below = tsend(grad_out, Y_SWAP), tsend(grad_out, X_DOWN), tsend(grad_out, X_UP)
    other, above, below, down_in, gate_in, up_pre = together(
        other, above, below, tsend(w_down, CORE), tsend(gate_pre, CORE), up_pre
    )
    near = [grad_out, other, above, below]
    above_y, below_y = tsend(other, X_DOWN), tsend(other, X_UP)
    far = [tsend(above[:part], X_DOWN), tsend(below[part:], X_UP)]
    up_in = tsend(up_pre, CORE)
    downs, pre = (w_down, down_in), (gate_pre, gate_in, up_pre, up_in)
    firsts = slope_call(table, 0, near, downs, pre, 4)
    hidden = hidden_call(table, pre, step, 1)

    above_y, below_y, far, inputs, _, _ = together(above_y, below_y, far, inputs, firsts[0], hidden)
    far_y = [tsend(above_y[:part], X_DOWN), tsend(below_y[part:], X_UP)]
    above_in, below_in, other_in = tsend(inputs, X_DOWN), tsend(inputs, X_UP), tsend(inputs, Y_SWAP)
    last = [above_y, below_y, *far, *far_y]
    down_own, down_other = weight_call(table, 0, NZ, near + last, [(hidden,)], 12)
    down_other = tsend(down_other, CORE)
    above_in, below_in, other_in, w_gate, w_up, _ = together(above_in, below_in, other_in, w_gate, w_up, down_own)

    rows_in = [inputs, other_in, above_in, below_in]
    above_y, below_y = tsend(other_in, X_DOWN), tsend(other_in, X_UP)
    w_gate_in, w_up_in = tsend(w_gate, CORE), tsend(w_up, CORE)
    seconds = slope_call(table, CHUNKS // 2, last, after(downs, above_in, below_in, down_own), pre, 12)
    above_y, below_y, below_in, w_gate_in, w_up_in = together(above_y, below_y, below_in, w_gate_in, w_up_in)
    far, far_y = tsend(below_in, X_UP), tsend(above_y, X_DOWN)
    rows_in += [above_y, below_y, far, far_y]
    d_gate, d_up = zip(firsts, seconds)
    partial = input_call(*after((d_gate, d_up), down_other, above_y, below_y), (w_gate, w_gate_in, w_up, w_up_in), 12)
    far_down, one_down, three_down, rest_down = split(down_own + down_other)
    far_down, one_down, three_down = dsend(low(far_down), Z_FAR), dsend(low(one_down), Z_UP), dsend(low(three_down), Z_DOWN)

    d_gate, d_up = after((d_gate, d_up), partial[0, 0], far_down, one_down, three_down)
    far_own, far_other = weight_call(table, 0, 1, rows_in, (d_gate, d_up), 0.1)
    far_other = tsend(far_other, CORE)
    one, three = tsend(after(partial[1, 2], far), X_UP), tsend(after(partial[1, 3], far_y), X_DOWN)
    d_gate, d_up = after((d_gate, d_up), far_own, far_other)
    ring_own, ring_other = weight_call(table, 1, 2, rows_in, (d_gate, d_up), 12)
    far_sum = low(far_own + far_other)
    far_up, far_dn = dsend(far_sum[0], Z_UP), dsend(far_sum[1], Z_DOWN)
    one, three, below, _ = together(one, three, partial[0, 2], ring_own)
    above, below = tsend(low(partial[1, 1] + one), X_UP), tsend(below, X_DOWN)
    far_up, far_dn, ring_other = together(far_up, far_dn, ring_other)
    above, below, up = together(above, below, partial[0, 1])
    d_gate, d_up = after((d_gate, d_up), ring_own)
    rest_own, rest_other = weight_call(table, 3, 1, rows_in, (d_gate, d_up), 12)
    ring_up, ring_dn = ring_call(ring_own, tsend(ring_other, CORE), *after((far_up, far_dn), rest_own))
    rest_other = tsend(rest_other, CORE)
    ring_up, ring_dn = dsend(ring_up, Z_UP), dsend(ring_dn, Z_DOWN)
    total = tsend(low(after(partial[1, 0], rest_other) + above + three), Y_SWAP)
    below, up = tsend(low(partial[0, 3] + below), X_DOWN), tsend(up, X_UP)
    ring_up, ring_dn, below, up, rest_down = together(ring_up, ring_dn, below, up, rest_down)
    rest_down = rest_down + one_down + three_down + far_down
    rest = rest_own + rest_other + ring_up + ring_dn
    d_input = partial[0, 0] + below + up + total
    down_part = (rest_down[0] + dsend(low(rest_down[1]), F_SWAP)).T
    both_part = rest[0] + dsend(low(rest[1]), F_SWAP)
    return (d_input, both_part[:, :width], both_part[:, width:], down_part)


def solution(mesh):
    in_specs = (
        P(("dp", "tensor"), None),
        P(("dp", "tensor"), None),
        P("dp", "tensor"),
        P("dp", "tensor"),
        P(None, "tensor"),
        P(None, "tensor"),
        P("tensor", None),
    )
    out_specs = (P(("dp", "tensor"), None), P("dp", "tensor"), P("dp", "tensor"), P("tensor", "dp"))
    return jax.shard_map(
        on_device, mesh=mesh, in_specs=in_specs, out_specs=out_specs, check_vma=False
    )
```

```python
import jax
import jax.numpy as jnp
import numpy as np
from jax import lax
from jax.experimental import pallas as pl
from jax.experimental.pallas import tpu as pltpu
from jax.sharding import PartitionSpec as P

NY, NX, NC = 2, 4, 2
NZ, NF = 4, 2
BF, F32 = jnp.bfloat16, jnp.float32
ORDER = [(0, 0), (1, 0), (0, 1), (0, 3), (1, 1), (1, 3), (0, 2), (1, 2)]
CHUNKS = len(ORDER)


def tensor_pairs(move):
    index = lambda y, x, c: (y * NX + x) * NC + c
    return [(index(y, x, c), index(*move(y, x, c))) for y in range(NY) for x in range(NX) for c in range(NC)]


def dp_pairs(move):
    index = lambda z, f: z * NF + f
    return [(index(z, f), index(*move(z, f))) for z in range(NZ) for f in range(NF)]


CORE = tensor_pairs(lambda y, x, c: (y, x, 1 - c))
Y_SWAP = tensor_pairs(lambda y, x, c: (1 - y, x, c))
X_UP = tensor_pairs(lambda y, x, c: (y, (x + 1) % NX, c))
X_DOWN = tensor_pairs(lambda y, x, c: (y, (x - 1) % NX, c))
Z_UP = dp_pairs(lambda z, f: ((z + 1) % NZ, f))
Z_DOWN = dp_pairs(lambda z, f: ((z - 1) % NZ, f))
Z_FAR = dp_pairs(lambda z, f: ((z + 2) % NZ, f))
F_SWAP = dp_pairs(lambda z, f: (z, 1 - f))

FARTHEST = (2, 1, 3, 0)
ROWS = np.array(
    [
        [((y ^ dy) * NX + (x + dx) % NX) * NC + c for dy, dx in ORDER]
        for y in range(NY) for x in range(NX) for c in range(NC)
    ],
    np.int32,
)
SLABS = np.array([[*((z + dz) % NZ for dz in FARTHEST), f] for z in range(NZ) for f in range(NF)], np.int32)
ANY = pl.BlockSpec(memory_space=pltpu.HBM)
VMEM = pl.BlockSpec(memory_space=pltpu.VMEM)
NT = (((1,), (1,)), ((), ()))
TN = (((0,), (0,)), ((), ()))


def tsend(value, pairs):
    return lax.ppermute(value, "tensor", pairs)


def dsend(value, pairs):
    return lax.ppermute(value, "dp", pairs)


def low(value):
    return value.astype(BF)


def params():
    return pltpu.CompilerParams(vmem_limit_bytes=20 << 20)


def cost(effort, flops, moved):
    return pl.CostEstimate(flops=int(flops * effort), bytes_accessed=int(moved * effort), transcendentals=0)


def hidden_body(table_ref, *refs):
    pre, (out,) = refs[:4], refs[4:]
    width = pre[0].shape[1]
    for core in range(NC):
        gate, upper = pre[core][...].astype(F32), pre[NC + core][...].astype(F32)
        out[:, core * width : (core + 1) * width] = (gate / (1.0 + jnp.exp(-gate)) * upper).astype(BF)


def hidden_call(table, pre, step, effort):
    width = pre[0].shape[1]
    total, both = step * CHUNKS, NC * width
    return pl.pallas_call(
        hidden_body,
        out_shape=jax.ShapeDtypeStruct((total, both), BF),
        grid_spec=pltpu.PrefetchScalarGridSpec(
            num_scalar_prefetch=1,
            grid=(CHUNKS,),
            in_specs=[pl.BlockSpec((step, width), lambda k, t: (t[k], 0))] * 4,
            out_specs=pl.BlockSpec((step, both), lambda k, t: (k, 0)),
        ),
        compiler_params=params(),
        cost_estimate=cost(effort, 16 * total * both, 6 * total * both),
        name="hidden",
    )(table, *pre)


def slope_body(first, count, table_ref, *refs):
    chunks, refs = refs[:count], refs[count:]
    down_pair, pre, (dgate_ref, dup_ref) = refs[:2], refs[2:6], refs[6:8]
    cot, down, gates, uppers, chunk_sem, down_sem, pre_sem = refs[8:]
    step = cot.shape[0] // (CHUNKS // 2)
    width = pre[0].shape[1]
    starts = np.cumsum([0] + [c.shape[0] for c in chunks]).tolist()

    def down_copy(j):
        return pltpu.make_async_copy(down_pair[j], down.at[pl.ds(j * width, width)], down_sem.at[j])

    def chunk_copy(k):
        return pltpu.make_async_copy(chunks[k], cot.at[pl.ds(starts[k], chunks[k].shape[0])], chunk_sem.at[k])

    def pre_copy(k, j):
        target = (gates, uppers)[j // 2]
        return pltpu.make_async_copy(
            pre[j].at[pl.ds(table_ref[first + k] * step, step)],
            target.at[pl.ds(k * step, step), pl.ds((j % 2) * width, width)],
            pre_sem.at[k, j],
        )

    for j in range(2):
        down_copy(j).start()
    for k in range(count):
        chunk_copy(k).start()
    for k in range(CHUNKS // 2):
        for j in range(4):
            pre_copy(k, j).start()
    for j in range(2):
        down_copy(j).wait()
    tile = 2 * step
    for i in range(CHUNKS // 4):
        for k in range(count):
            if i * tile <= starts[k] < (i + 1) * tile:
                chunk_copy(k).wait()
        for k in (2 * i, 2 * i + 1):
            for j in range(4):
                pre_copy(k, j).wait()
        at = pl.ds(i * tile, tile)
        d_hidden = lax.dot_general(cot[at, :], down[...], NT, preferred_element_type=F32)
        gate = gates[at, :].astype(F32)
        sig = 1.0 / (1.0 + jnp.exp(-gate))
        dgate_ref[at, :] = (d_hidden * uppers[at, :].astype(F32) * sig * (1.0 + gate * (1.0 - sig))).astype(BF)
        dup_ref[at, :] = (d_hidden * (gate * sig)).astype(BF)


def slope_call(table, first, chunks, downs, pre, effort):
    count = len(chunks)
    total, depth = sum(c.shape[0] for c in chunks), chunks[0].shape[1]
    width = downs[0].shape[0]
    both = NC * width
    out = jax.ShapeDtypeStruct((total, both), BF)
    return pl.pallas_call(
        lambda *refs: slope_body(first, count, *refs),
        out_shape=(out, out),
        grid_spec=pltpu.PrefetchScalarGridSpec(
            num_scalar_prefetch=1,
            grid=(1,),
            in_specs=[ANY] * (count + 6),
            out_specs=[pl.BlockSpec((total, both), lambda i, t: (0, 0))] * 2,
            scratch_shapes=[
                pltpu.VMEM((total, depth), BF),
                pltpu.VMEM((both, depth), BF),
                pltpu.VMEM((total, both), BF),
                pltpu.VMEM((total, both), BF),
                pltpu.SemaphoreType.DMA((count,)),
                pltpu.SemaphoreType.DMA((2,)),
                pltpu.SemaphoreType.DMA((CHUNKS // 2, 4)),
            ],
        ),
        compiler_params=params(),
        cost_estimate=cost(effort, 2 * total * depth * both, 8 << 20),
        name="slope",
    )(table, *chunks, *downs, *pre)


def weight_body(count, wide, table_ref, *refs):
    chunks, rights, (own_ref, other_ref) = refs[:count], refs[count:-2], refs[-2:]
    parts = len(rights) // wide
    features = own_ref.shape[1]
    width = own_ref.shape[2] // wide
    far = table_ref[CHUNKS + NZ]
    starts = np.cumsum([0] + [c.shape[0] for c in chunks]).tolist()
    per = starts[-1] // parts
    lefts = [
        jnp.concatenate([c[...] for c, start in zip(chunks, starts) if p * per <= start < (p + 1) * per], axis=0)
        for p in range(parts)
    ]
    for w in range(wide):
        both = None
        for p in range(parts):
            term = lax.dot_general(lefts[p], rights[w * parts + p][...], TN, preferred_element_type=F32)
            both = term if both is None else both + term
        at = pl.ds(w * width, width)
        for f in range(NF):
            slab = both[f * features : (f + 1) * features]
            own_ref[f ^ far, :, at] = slab[:, :width]
            other_ref[f ^ far, :, at] = slab[:, width:].astype(BF)


def weight_call(table, first, blocks, chunks, rights, effort):
    count, wide, parts = len(chunks), len(rights), len(rights[0])
    rows, both = rights[0][0].shape
    depth = chunks[0].shape[1]
    features = depth // (NZ * NF)
    slab = (blocks * NF, features, wide * both // NC)
    block = pl.BlockSpec((NF, *slab[1:]), lambda r, t: (r, 0, 0))
    return pl.pallas_call(
        lambda *refs: weight_body(count, wide, *refs),
        out_shape=(jax.ShapeDtypeStruct(slab, F32), jax.ShapeDtypeStruct(slab, BF)),
        grid_spec=pltpu.PrefetchScalarGridSpec(
            num_scalar_prefetch=1,
            grid=(blocks,),
            in_specs=[pl.BlockSpec((c.shape[0], NF * features), lambda r, t: (0, t[CHUNKS + first + r])) for c in chunks]
            + [pl.BlockSpec((rows, both), lambda r, t: (0, 0))] * (wide * parts),
            out_specs=[block, block],
        ),
        compiler_params=params(),
        cost_estimate=cost(effort, 2 * blocks * NF * features * rows * parts * both * wide, 10 << 20),
        name="weight",
    )(table, *chunks, *[part for right in rights for part in right])


def ring_body(own_up, own_down, in_up, in_down, far_up, far_down, up_ref, down_ref):
    up = own_up[...] + in_up[...].astype(F32)
    down = own_down[...] + in_down[...].astype(F32)

    @pl.when(pl.program_id(0) == 0)
    def _():
        up_ref[...] = (up + far_up[...].astype(F32)).astype(BF)
        down_ref[...] = down.astype(BF)

    @pl.when(pl.program_id(0) == 1)
    def _():
        up_ref[...] = up.astype(BF)
        down_ref[...] = (down + far_down[...].astype(F32)).astype(BF)


def ring_call(own, other, far_up, far_down):
    _, features, width = own.shape
    first = pl.BlockSpec((1, features, width), lambda f: (f, 0, 0))
    second = pl.BlockSpec((1, features, width), lambda f: (NF + f, 0, 0))
    whole = pl.BlockSpec((1, features, width), lambda f: (0, 0, 0))
    out = jax.ShapeDtypeStruct((NF, features, width), BF)
    return pl.pallas_call(
        ring_body,
        out_shape=(out, out),
        grid=(NF,),
        in_specs=[first, second, first, second, whole, whole],
        out_specs=[first, first],
        compiler_params=params(),
        cost_estimate=cost(1, 8 * own.size, 8 * own.size),
        name="ring",
    )(own, own, other, other, far_up[None], far_down[None])


KEPT = [(0, 0), (1, 0), (1, 1), (0, 3)]


def input_body(parts, *refs):
    lefts, weights, outs = refs[: 2 * parts], refs[2 * parts : 2 * parts + 4], refs[2 * parts + 4 :]
    step = outs[0].shape[0]
    gate_weight = jnp.concatenate([weights[0][...], weights[1][...]], axis=1)
    up_weight = jnp.concatenate([weights[2][...], weights[3][...]], axis=1)
    per = CHUNKS // parts
    for p in range(parts):
        total = lax.dot_general(lefts[p][...], gate_weight, NT, preferred_element_type=F32)
        total = total + lax.dot_general(lefts[parts + p][...], up_weight, NT, preferred_element_type=F32)
        for k in range(per):
            out = outs[p * per + k]
            out[...] = total[k * step : (k + 1) * step].astype(out.dtype)


def input_call(d_gates, d_ups, weights, effort):
    depth, width = weights[0].shape
    parts = len(d_gates)
    rows, both = d_gates[0].shape
    step = rows * parts // CHUNKS
    tile = 512
    outs = pl.pallas_call(
        lambda *refs: input_body(parts, *refs),
        out_shape=[jax.ShapeDtypeStruct((step, depth), F32 if o in KEPT else BF) for o in ORDER],
        grid=(depth // tile,),
        in_specs=[pl.BlockSpec((rows, both), lambda n: (0, 0))] * (2 * parts)
        + [pl.BlockSpec((tile, width), lambda n: (n, 0))] * 4,
        out_specs=[pl.BlockSpec((step, tile), lambda n: (0, n))] * CHUNKS,
        compiler_params=params(),
        cost_estimate=cost(effort, 4 * rows * parts * depth * both, 14 << 20),
        name="input",
    )(*d_gates, *d_ups, *weights)
    return dict(zip(ORDER, outs))


def after(values, *events):
    return lax.optimization_barrier((values, events))[0]


def split(slabs):
    return slabs.reshape(-1, NF, *slabs.shape[1:])


def on_device(inputs, grad_out, gate_pre, up_pre, w_gate, w_up, w_down):
    table = jnp.concatenate([jnp.asarray(ROWS)[lax.axis_index("tensor")], jnp.asarray(SLABS)[lax.axis_index("dp")]])
    step, width = grad_out.shape[0], w_down.shape[0]
    part = step // 2
    together = lambda *values: lax.optimization_barrier(values)

    other, above, below = tsend(grad_out, Y_SWAP), tsend(grad_out, X_DOWN), tsend(grad_out, X_UP)
    other, above, below, down_in, gate_in, up_pre = together(
        other, above, below, tsend(w_down, CORE), tsend(gate_pre, CORE), up_pre
    )
    near = [grad_out, other, above, below]
    above_y, below_y = tsend(other, X_DOWN), tsend(other, X_UP)
    far = [tsend(above[:part], X_DOWN), tsend(below[part:], X_UP)]
    up_in = tsend(up_pre, CORE)
    downs, pre = (w_down, down_in), (gate_pre, gate_in, up_pre, up_in)
    firsts = slope_call(table, 0, near, downs, pre, 4)
    hidden = hidden_call(table, pre, step, 1)

    above_y, below_y, far, inputs, _, _ = together(above_y, below_y, far, inputs, firsts[0], hidden)
    far_y = [tsend(above_y[:part], X_DOWN), tsend(below_y[part:], X_UP)]
    above_in, below_in, other_in = tsend(inputs, X_DOWN), tsend(inputs, X_UP), tsend(inputs, Y_SWAP)
    last = [above_y, below_y, *far, *far_y]
    down_own, down_other = weight_call(table, 0, NZ, near + last, [(hidden,)], 12)
    down_other = tsend(down_other, CORE)
    above_in, below_in, other_in, w_gate, w_up, _ = together(above_in, below_in, other_in, w_gate, w_up, down_own)

    rows_in = [inputs, other_in, above_in, below_in]
    above_y, below_y = tsend(other_in, X_DOWN), tsend(other_in, X_UP)
    w_gate_in, w_up_in = tsend(w_gate, CORE), tsend(w_up, CORE)
    seconds = slope_call(table, CHUNKS // 2, last, after(downs, above_in, below_in, down_own), pre, 12)
    above_y, below_y, below_in, w_gate_in, w_up_in = together(above_y, below_y, below_in, w_gate_in, w_up_in)
    far, far_y = tsend(below_in, X_UP), tsend(above_y, X_DOWN)
    rows_in += [above_y, below_y, far, far_y]
    d_gate, d_up = zip(firsts, seconds)
    partial = input_call(*after((d_gate, d_up), down_other, above_y, below_y), (w_gate, w_gate_in, w_up, w_up_in), 12)
    far_down, one_down, three_down, rest_down = split(down_own + down_other)
    far_down, one_down, three_down = dsend(low(far_down), Z_FAR), dsend(low(one_down), Z_UP), dsend(low(three_down), Z_DOWN)

    d_gate, d_up = after((d_gate, d_up), partial[0, 0], far_down, one_down, three_down)
    far_own, far_other = weight_call(table, 0, 1, rows_in, (d_gate, d_up), 0.1)
    far_other = tsend(far_other, CORE)
    one, three = tsend(after(partial[1, 2], far), X_UP), tsend(after(partial[1, 3], far_y), X_DOWN)
    d_gate, d_up = after((d_gate, d_up), far_own, far_other)
    ring_own, ring_other = weight_call(table, 1, 2, rows_in, (d_gate, d_up), 12)
    far_sum = low(far_own + far_other)
    far_up, far_dn = dsend(far_sum[0], Z_UP), dsend(far_sum[1], Z_DOWN)
    one, three, below, _ = together(one, three, partial[0, 2], ring_own)
    above, below = tsend(low(partial[1, 1] + one), X_UP), tsend(below, X_DOWN)
    far_up, far_dn, ring_other = together(far_up, far_dn, ring_other)
    above, below, up = together(above, below, partial[0, 1])
    d_gate, d_up = after((d_gate, d_up), ring_own)
    rest_own, rest_other = weight_call(table, 3, 1, rows_in, (d_gate, d_up), 12)
    ring_up, ring_dn = ring_call(ring_own, tsend(ring_other, CORE), *after((far_up, far_dn), rest_own))
    rest_other = tsend(rest_other, CORE)
    ring_up, ring_dn = dsend(ring_up, Z_UP), dsend(ring_dn, Z_DOWN)
    total = tsend(low(after(partial[1, 0], rest_other) + above + three), Y_SWAP)
    below, up = tsend(low(partial[0, 3] + below), X_DOWN), tsend(up, X_UP)
    ring_up, ring_dn, below, up, rest_down = together(ring_up, ring_dn, below, up, rest_down)
    rest_down = rest_down + one_down + three_down + far_down
    rest = rest_own + rest_other + ring_up + ring_dn
    d_input = partial[0, 0] + below + up + total
    down_part = (rest_down[0] + dsend(low(rest_down[1]), F_SWAP)).T
    both_part = rest[0] + dsend(low(rest[1]), F_SWAP)
    return (d_input, both_part[:, :width], both_part[:, width:], down_part)


def solution(mesh):
    in_specs = (
        P(("dp", "tensor"), None),
        P(("dp", "tensor"), None),
        P("dp", "tensor"),
        P("dp", "tensor"),
        P(None, "tensor"),
        P(None, "tensor"),
        P("tensor", None),
    )
    out_specs = (P(("dp", "tensor"), None), P("dp", "tensor"), P("dp", "tensor"), P("tensor", "dp"))
    return jax.shard_map(
        on_device, mesh=mesh, in_specs=in_specs, out_specs=out_specs, check_vma=False
    )
```
